32 devices in a mesh: facet: 8 (over y, x, core), col: 4 (over z).
Axes of the slice: x: 2, y: 2, z: 4, core: 2. Of those that a mesh axis runs over, the one named last changes fastest.
Arguments:
- facets: float32 [2, 8, 24, 2, 4096], P(None, 'facet', None, None, 'col'), may hold values from -6 to 6
- facet_x: int32 [8], P('facet'), may hold values from 0 to 32767
- facet_y: int32 [2], replicated, may hold values from 0 to 32767
- col_u: int32 [8], replicated, may hold values from 0 to 32767
- slot_col: int32 [4, 8], P('col'), may hold values from 0 to 1
- slot_v: int32 [4, 8], P('col'), may hold values from 0 to 32767
Outputs:
- subgrids: float32 [4, 8, 512, 1024], P('col', 'facet')
The draws below stay inside these ranges and needn't reach their ends.
Inputs may be any that keep to these rules, and one draw needn't show every extreme that they name: `col_u`: offset in the image. `slot_col`: the subgrid's column is owner * 2 + this value. `slot_v`: offset in the image.
All inputs are finite; a program needn't handle non-finite values.
Results may differ from the reference program's by a relative error of at most 0.0003.
Values sent between devices are 32-bit elements; how exact they have to be, the bound alone decides.
A program may use at most 128 MiB of HBM per device.

```python
import math
import jax
import jax.numpy as jnp
from jax import lax

FS = 4096
SG = 512
BAND = 24
COLS_DEV = 2
NFC = 8
NCOL = 8
CAP = 8
IMG = 32768
N_FACET = 8
N_COL = 4


def with_ends(array, key, least, largest):
    longest = array.shape.index(max(array.shape))
    spots = []
    for shift in (0, 1):
        where = [jax.random.randint(jax.random.fold_in(key, axis), (), 0, length) for axis, length in enumerate(array.shape)]
        where[longest] = (where[longest] + shift) % array.shape[longest]
        spots.append(tuple(where))
    return array.at[spots[0]].set(least).at[spots[1]].set(largest)


def block_levels(stream_key, dims, cuts, low, high):
    def one(axis_at, shards_of):
        heights = jax.random.uniform(jax.random.fold_in(jax.random.fold_in(stream_key, 6), axis_at), (shards_of,), jnp.float32, low / len(cuts), high / len(cuts))
        return jnp.repeat(jnp.exp(heights), dims[axis_at] // shards_of).reshape((-1,) + (1,) * (len(dims) - axis_at - 1))

    factor_of = one(*cuts[0])
    for cut in cuts[1:]:
        factor_of = factor_of * one(*cut)
    return factor_of


def scatter_about(own_key, shape, deviation, reach, cuts=(), kind=jnp.bfloat16):
    entries = deviation * jax.random.normal(own_key, shape, jnp.float32)
    if cuts:
        entries = entries * block_levels(own_key, shape, cuts, -0.22, 0.18)
    return jnp.clip(entries, -reach, reach).astype(kind)


def setup_inputs(seed: int = 0) -> dict:
    seeds = jax.random.split(jax.random.key(seed), 7)
    return {
        "facets": scatter_about(seeds[0], (2, NFC, BAND, 2, FS), 1.0, 6.0, ((1, 8), (4, 4)), jnp.float32),
        "facet_x": with_ends(jax.random.randint(seeds[1], (NFC,), 0, IMG), jax.random.fold_in(seeds[1], 1), 0, IMG - 1).astype(jnp.int32),
        "facet_y": jax.random.randint(seeds[2], (2,), 0, IMG).astype(jnp.int32),
        "col_u": with_ends(jax.random.randint(seeds[3], (NCOL,), 0, IMG), jax.random.fold_in(seeds[3], 1), 0, IMG - 1).astype(jnp.int32),
        "slot_col": with_ends(jax.random.randint(seeds[4], (N_COL, CAP), 0, COLS_DEV), jax.random.fold_in(seeds[4], 1), 0, COLS_DEV - 1).astype(jnp.int32),
        "slot_v": with_ends(jax.random.randint(seeds[5], (N_COL, CAP), 0, IMG), jax.random.fold_in(seeds[5], 1), 0, IMG - 1).astype(jnp.int32),
    }


def mulmod(first_factor, second_factor, modulus):
    upper = first_factor * (second_factor // 512) % modulus
    return (upper * 512 + first_factor * (second_factor % 512)) % modulus

def reference(facets, facet_x, facet_y, col_u, slot_col, slot_v):
    img = FS * N_FACET
    turn = 2.0 * math.pi / img
    cells = (col_u[:, None] + jnp.arange(SG, dtype=jnp.int32)[None, :]) % img
    flat_cells = cells.reshape(-1).astype(jnp.int32)

    def add_facet(carry, index):
        block = lax.dynamic_index_in_dim(facets, index, 1, keepdims=False)
        signal = block[:, :, 0, :] + 1j * block[:, :, 1, :]
        spectrum = jnp.fft.fft(signal, n=img, axis=-1)
        picked = spectrum[:, :, flat_cells]
        offset_x = lax.dynamic_index_in_dim(facet_x, index, 0, keepdims=False)
        angle = mulmod(flat_cells, offset_x, img).astype(jnp.float32) * turn
        cosine = jnp.cos(angle)
        sine = jnp.sin(angle)
        real_in = jnp.real(picked)
        imag_in = jnp.imag(picked)
        new_real = real_in * cosine + imag_in * sine
        new_imag = imag_in * cosine - real_in * sine
        return ((carry[0] + new_real, carry[1] + new_imag), None)
    zeros = jnp.zeros((2, BAND, NCOL * SG), jnp.float32)
    (sum_real, sum_imag), unused_out = lax.scan(add_facet, (zeros, zeros), jnp.arange(N_FACET, dtype=jnp.int32))
    summed = jnp.concatenate([sum_real.reshape(2 * BAND, NCOL, SG), sum_imag.reshape(2 * BAND, NCOL, SG)], axis=-1)
    row_ids = jnp.arange(2 * BAND, dtype=jnp.int32)
    y_start = jnp.where(row_ids // BAND == 0, facet_y[0], facet_y[1])
    row_cells = (y_start + row_ids % BAND) % img
    scale = 1.0 / math.sqrt(2.0 * FS * BAND * N_FACET)
    flat_col = slot_col.reshape(-1)
    flat_v = slot_v.reshape(-1)

    def one_slot(slot_id):
        owner = slot_id // CAP
        column = (owner * COLS_DEV + flat_col[slot_id]).astype(jnp.int32)
        shift_v = flat_v[slot_id]
        v_cells = (shift_v + jnp.arange(SG, dtype=jnp.int32)) % img
        angle = mulmod(v_cells[:, None], row_cells[None, :], img).astype(jnp.float32) * turn
        cosine = jnp.cos(angle)
        sine = jnp.sin(angle)
        chosen = lax.dynamic_index_in_dim(summed, column, 1, keepdims=False)
        first = jnp.dot(cosine, chosen, precision=lax.Precision.HIGHEST, preferred_element_type=jnp.float32)
        second = jnp.dot(sine, chosen, precision=lax.Precision.HIGHEST, preferred_element_type=jnp.float32)
        real_out = first[:, :SG] + second[:, SG:]
        imag_out = first[:, SG:] - second[:, :SG]
        return jnp.concatenate([real_out, imag_out], axis=-1) * scale
    result = lax.map(one_slot, jnp.arange(N_COL * CAP, dtype=jnp.int32))
    return result.reshape(N_COL, CAP, SG, 2 * SG)
```

```python
import functools
import math

import jax
import jax.numpy as jnp
from jax import lax
from jax.experimental import pallas as pl
from jax.experimental.pallas import tpu as pltpu
from jax.sharding import PartitionSpec as P

SG = 512
HALF = SG // 2
COLS_DEV = 2
F32 = jnp.float32
BF16 = jnp.bfloat16
I32 = jnp.int32
MESH = pl.DeviceIdType.MESH


def turn(m, mod):
    bits = mod.bit_length() - 1
    m = m & (mod - 1)
    quad = lax.shift_right_logical(m + (mod >> 3), jnp.int32(bits - 2))
    rest = m - lax.shift_left(quad, jnp.int32(bits - 2))
    t = rest.astype(F32) * F32(2.0 * math.pi / mod)
    t2 = t * t
    sine = t + t * t2 * (F32(-1 / 6) + t2 * (F32(1 / 120) + t2 * F32(-1 / 5040)))
    cosine = F32(1.0) + t2 * (
        F32(-0.5) + t2 * (F32(1 / 24) + t2 * (F32(-1 / 720) + t2 * F32(1 / 40320)))
    )
    odd = (quad & 1) == 1
    c = jnp.where(odd, sine, cosine)
    s = jnp.where(odd, cosine, sine)
    c = jnp.where(((quad + 1) & 2) == 2, -c, c)
    s = jnp.where((quad & 2) == 2, -s, s)
    return c, s


def split(value):
    high = value.astype(BF16)
    return high, (value - high.astype(F32)).astype(BF16)


def mm(a, b):
    return jnp.dot(a, b, preferred_element_type=F32)


def gather_kernel(
    nf, nc, img, band,
    fx_ref, fy_ref, u_ref, sc_ref, sv_ref, ucol_ref, facets_ref,
    h_ref, e_ref,
    cells, fxs, fxall, table, premod, zbuf, part, zrecv, total, gat,
    s_a2a, r_a2a, s_fx, r_fx, s_z, r_z, s_g, r_g, l_sem,
):
    f = lax.axis_index("facet")
    c = lax.axis_index("col")
    rows = facets_ref.shape[0]
    rpd = rows // nf
    width = facets_ref.shape[-1]
    mod = 2 * img
    ncell = COLS_DEV * rpd
    pad = h_ref.shape[0] // nf

    fxs[...] = jnp.full(fxs.shape, fx_ref[0], I32)
    barrier = pltpu.get_barrier_semaphore()
    for d in range(1, nf):
        pl.semaphore_signal(barrier, inc=1, device_id=(lax.rem(f + d, nf), c), device_id_type=MESH)
    for d in range(1, nc):
        pl.semaphore_signal(barrier, inc=1, device_id=(f, lax.rem(c + d, nc)), device_id_type=MESH)
    pl.semaphore_wait(barrier, nf + nc - 2)

    sends = []
    for d in range(1, nf):
        peer = lax.rem(f + d, nf)
        copy = pltpu.make_async_remote_copy(
            src_ref=facets_ref.at[pl.ds(peer * rpd, rpd)],
            dst_ref=cells.at[:, :, f],
            send_sem=s_a2a.at[d], recv_sem=r_a2a.at[d],
            device_id=(peer, c), device_id_type=MESH,
        )
        copy.start()
        small = pltpu.make_async_remote_copy(
            src_ref=fxs, dst_ref=fxall.at[f],
            send_sem=s_fx.at[d], recv_sem=r_fx.at[d],
            device_id=(peer, c), device_id_type=MESH,
        )
        small.start()
        sends += [copy, small]
    own = pltpu.make_async_copy(facets_ref.at[pl.ds(f * rpd, rpd)], cells.at[:, :, f], l_sem.at[0])
    own.start()
    own_fx = pltpu.make_async_copy(fxs, fxall.at[f], l_sem.at[1])
    own_fx.start()

    start = c * width
    block = 64

    def table_step(i, carry):
        first = pl.multiple_of(i * block, block)
        x = lax.broadcasted_iota(I32, (block, HALF), 0) + (start + first)
        j = lax.broadcasted_iota(I32, (block, HALF), 1)
        cosine, sine = turn((2 * j + 1) * x, mod)
        ch, cl = split(cosine)
        sh, sl = split(sine)
        table[0, pl.ds(first, block), pl.ds(0, HALF)] = ch
        table[0, pl.ds(first, block), pl.ds(HALF, HALF)] = sh
        table[1, pl.ds(first, block), pl.ds(0, HALF)] = cl
        table[1, pl.ds(first, block), pl.ds(HALF, HALF)] = sl
        return carry

    lax.fori_loop(0, width // block, table_step, 0)
    ucol = ucol_ref[...]
    xs = lax.broadcasted_iota(I32, (ucol.shape[0], width), 1) + start
    pc, ps = turn((2 * ucol + (SG - 1)) * xs, mod)
    premod[0] = pc
    premod[1] = ps

    scale = 1.0 / math.sqrt(1.0 * rows * width * nc * nf)
    shift_v = jnp.full((1, 1), sv_ref[f], I32)
    chosen = jnp.full((1, 1), sc_ref[f], I32)
    fy0 = jnp.full((1, 1), fy_ref[0], I32)
    fy1 = jnp.full((1, 1), fy_ref[1], I32)

    def v_step(i, carry):
        first = pl.multiple_of(i * block, block)
        b = lax.broadcasted_iota(I32, (block, nf * pad), 0) + first
        q = lax.broadcasted_iota(I32, (1, nf * pad), 1)
        inner = lax.rem(q, pad)
        peer = lax.div(q, pad)
        column = lax.div(inner, rpd)
        g = peer * rpd + lax.rem(inner, rpd)
        cell = jnp.where(g < band, fy0 + g, fy1 + g - band)
        use = (inner < ncell) & (column == chosen)
        cosine, sine = turn(2 * (shift_v + b) * cell, mod)
        weight = jnp.where(use, F32(scale), F32(0.0))
        e_ref[pl.ds(first, block), pl.ds(0, nf * pad)] = cosine * weight
        e_ref[pl.ds(first, block), pl.ds(nf * pad, nf * pad)] = sine * weight
        return carry

    lax.fori_loop(0, SG // block, v_step, 0)
    h_ref[...] = jnp.zeros_like(h_ref)

    own.wait()
    own_fx.wait()
    for copy in sends:
        copy.wait()

    fx = fxall[:, 0, :]
    fx = jnp.concatenate([fx] * (SG // fx.shape[-1]), axis=1)
    lane = lax.broadcasted_iota(I32, (nf, SG), 1)
    a = jnp.where(lane < HALF, HALF + lane, SG - 1 - lane)

    zcopies = []
    for d in list(range(1, nc)) + [0]:
        owner = lax.rem(c + d, nc)
        for s in range(COLS_DEV):
            col = owner * COLS_DEV + s
            cosine = premod[0, pl.ds(col, 1), :].reshape(1, 1, width)
            sine = premod[1, pl.ds(col, 1), :].reshape(1, 1, width)
            re = cells[:, 0]
            im = cells[:, 1]
            zr = (re * cosine + im * sine).reshape(rpd * nf, width)
            zi = (im * cosine - re * sine).reshape(rpd * nf, width)
            for n, z in enumerate((zr, zi)):
                hi, lo = split(z)
                at = (s * 2 + n) * rpd * nf
                zbuf[0, pl.ds(at, rpd * nf), :] = hi
                zbuf[1, pl.ds(at, rpd * nf), :] = lo
        prod = mm(zbuf[0], table[0]) + mm(zbuf[1], table[0]) + mm(zbuf[0], table[1])
        for s in range(COLS_DEV):
            col = owner * COLS_DEV + s
            at = s * 2 * rpd * nf
            fr = prod[at:at + rpd * nf]
            fi = prod[at + rpd * nf:at + 2 * rpd * nf]
            rc, rs = fr[:, :HALF], fr[:, HALF:]
            ic, is_ = fi[:, :HALF], fi[:, HALF:]
            hr = jnp.concatenate([rc + is_, rc - is_], axis=1).reshape(rpd, nf, SG)
            hm = jnp.concatenate([ic - rs, ic + rs], axis=1).reshape(rpd, nf, SG)
            wc, ws = turn(2 * (a + u_ref[col]) * fx, mod)
            out_r = jnp.sum(hr * wc + hm * ws, axis=1)
            out_i = jnp.sum(hm * wc - hr * ws, axis=1)
            part[d, pl.ds(s * rpd, rpd), pl.ds(0, SG)] = out_r
            part[d, pl.ds(s * rpd, rpd), pl.ds(SG, SG)] = out_i
        if d:
            copy = pltpu.make_async_remote_copy(
                src_ref=part.at[d], dst_ref=zrecv.at[d],
                send_sem=s_z.at[d], recv_sem=r_z.at[d],
                device_id=(f, owner), device_id_type=MESH,
            )
            copy.start()
            zcopies.append(copy)

    acc = part[0]
    for d, copy in zip(range(1, nc), zcopies):
        copy.wait()
        acc = acc + zrecv[d]
    flip = lax.broadcasted_iota(I32, (HALF, HALF), 0) + lax.broadcasted_iota(I32, (HALF, HALF), 1)
    flip = jnp.where(flip == HALF - 1, F32(1.0), F32(0.0)).astype(BF16)
    for n in range(2):
        low = acc[:, n * SG + HALF:(n + 1) * SG]
        hi, lo = split(low)
        total[:, pl.ds(n * SG, HALF)] = mm(hi, flip) + mm(lo, flip)
        total[:, pl.ds(n * SG + HALF, HALF)] = acc[:, n * SG:n * SG + HALF]

    gcopies = []
    for d in range(1, nf):
        peer = lax.rem(f + d, nf)
        copy = pltpu.make_async_remote_copy(
            src_ref=total, dst_ref=gat.at[f],
            send_sem=s_g.at[d], recv_sem=r_g.at[d],
            device_id=(peer, c), device_id_type=MESH,
        )
        copy.start()
        gcopies.append(copy)
    own = pltpu.make_async_copy(total, gat.at[f], l_sem.at[2])
    own.start()
    own.wait()
    for copy in gcopies:
        copy.wait()
    for j in range(nf):
        h_ref[pl.ds(j * pad, ncell), :] = gat[j]


def v_kernel(h_ref, e_ref, out_ref, rhs_hi, rhs_lo):
    @pl.when(pl.program_id(0) == 0)
    def _():
        k = h_ref.shape[0]
        hi, lo = split(h_ref[...])
        for ref, h in ((rhs_hi, hi), (rhs_lo, lo)):
            ref[pl.ds(0, k), :] = h
            ref[pl.ds(k, k), pl.ds(0, SG)] = h[:, SG:]
            ref[pl.ds(k, k), pl.ds(SG, SG)] = -h[:, :SG]

    eh, el = split(e_ref[...])
    out_ref[...] = mm(eh, rhs_hi[...]) + mm(el, rhs_hi[...]) + mm(eh, rhs_lo[...])


def per_device(nf, nc, facets, facet_x, facet_y, col_u, slot_col, slot_v):
    width = facets.shape[-1]
    band = facets.shape[2]
    img = width * nc * nf
    rows = facets.shape[0] * band
    rpd = rows // nf
    ncol = COLS_DEV * nc
    ncell = COLS_DEV * rpd
    pad = -(-ncell // 16) * 16
    vm = pl.BlockSpec(memory_space=pltpu.VMEM)
    sm = pl.BlockSpec(memory_space=pltpu.SMEM)
    dma = pltpu.SemaphoreType.DMA
    h, e = pl.pallas_call(
        functools.partial(gather_kernel, nf, nc, img, band),
        out_shape=(
            jax.ShapeDtypeStruct((nf * pad, 2 * SG), F32),
            jax.ShapeDtypeStruct((SG, 2 * nf * pad), F32),
        ),
        in_specs=[sm, sm, sm, sm, sm, vm, pl.BlockSpec(memory_space=pl.ANY)],
        out_specs=(vm, vm),
        scratch_shapes=[
            pltpu.VMEM((rpd, 2, nf, width), F32),
            pltpu.VMEM((8, 128), I32),
            pltpu.VMEM((nf, 8, 128), I32),
            pltpu.VMEM((2, width, SG), BF16),
            pltpu.VMEM((2, ncol, width), F32),
            pltpu.VMEM((2, 2 * COLS_DEV * rpd * nf, width), BF16),
            pltpu.VMEM((nc, ncell, 2 * SG), F32),
            pltpu.VMEM((nc, ncell, 2 * SG), F32),
            pltpu.VMEM((ncell, 2 * SG), F32),
            pltpu.VMEM((nf, ncell, 2 * SG), F32),
            dma((nf,)), dma((nf,)), dma((nf,)), dma((nf,)),
            dma((nc,)), dma((nc,)), dma((nf,)), dma((nf,)), dma((3,)),
        ],
        compiler_params=pltpu.CompilerParams(collective_id=0, has_side_effects=True),
        name="gather_columns",
    )(
        facet_x, facet_y, col_u, slot_col[0], slot_v[0], col_u[:, None],
        facets.reshape(rows, 2, width),
    )
    tile = 128
    out = pl.pallas_call(
        v_kernel,
        grid=(SG // tile,),
        out_shape=jax.ShapeDtypeStruct((SG, 2 * SG), F32),
        in_specs=[
            pl.BlockSpec((nf * pad, 2 * SG), lambda i: (0, 0)),
            pl.BlockSpec((tile, 2 * nf * pad), lambda i: (i, 0)),
        ],
        out_specs=pl.BlockSpec((tile, 2 * SG), lambda i: (i, 0)),
        scratch_shapes=[
            pltpu.VMEM((2 * nf * pad, 2 * SG), BF16),
            pltpu.VMEM((2 * nf * pad, 2 * SG), BF16),
        ],
        name="v_transform",
    )(h, e)
    return out[None, None]


def solution(mesh):
    placed = (
        P(None, "facet", None, None, "col"),
        P("facet"),
        P(),
        P(),
        P("col", None),
        P("col", None),
    )
    return jax.shard_map(
        functools.partial(per_device, mesh.shape["facet"], mesh.shape["col"]),
        mesh=mesh,
        in_specs=placed,
        out_specs=P("col", "facet", None, None),
        check_vma=False,
    )
```

```python
import functools
import math

import jax
import jax.numpy as jnp
from jax import lax
from jax.experimental import pallas as pl
from jax.experimental.pallas import tpu as pltpu
from jax.sharding import PartitionSpec as P

SG = 512
HALF = SG // 2
COLS_DEV = 2
F32 = jnp.float32
BF16 = jnp.bfloat16
I32 = jnp.int32
MESH = pl.DeviceIdType.MESH


def turn(m, mod):
    bits = mod.bit_length() - 1
    m = m & (mod - 1)
    quad = lax.shift_right_logical(m + (mod >> 3), jnp.int32(bits - 2))
    rest = m - lax.shift_left(quad, jnp.int32(bits - 2))
    t = rest.astype(F32) * F32(2.0 * math.pi / mod)
    t2 = t * t
    sine = t + t * t2 * (F32(-1 / 6) + t2 * (F32(1 / 120) + t2 * F32(-1 / 5040)))
    cosine = F32(1.0) + t2 * (
        F32(-0.5) + t2 * (F32(1 / 24) + t2 * (F32(-1 / 720) + t2 * F32(1 / 40320)))
    )
    odd = (quad & 1) == 1
    c = jnp.where(odd, sine, cosine)
    s = jnp.where(odd, cosine, sine)
    c = jnp.where(((quad + 1) & 2) == 2, -c, c)
    s = jnp.where((quad & 2) == 2, -s, s)
    return c, s


def split(value):
    high = value.astype(BF16)
    return high, (value - high.astype(F32)).astype(BF16)


def mm(a, b):
    return jnp.dot(a, b, preferred_element_type=F32)


def partner(index, count, step):
    if count & (count - 1):
        return lax.rem(index + step, count)
    bit = 1
    while bit < count:
        if step & bit:
            index = index + bit - 2 * bit * lax.rem(lax.div(index, bit), 2)
        bit *= 2
    return index


def gather_kernel(
    nf, nc, img, band, cuts, hpad,
    fx_ref, fy_ref, u_ref, sc_ref, sv_ref, facets_ref,
    h_ref, e_ref,
    cells, fxs, fxall, table, premod, phase, zbuf, part, zrecv, gsend, gat,
    s_a2a, r_a2a, s_fx, r_fx, s_z, r_z, s_g, r_g, l_sem,
):
    f = lax.axis_index("facet")
    c = lax.axis_index("col")
    rows = facets_ref.shape[0]
    rpd = rows // nf
    width = facets_ref.shape[-1]
    mod = 2 * img
    ncol = COLS_DEV * nc
    depth = len(cuts) * nf * hpad

    fxs[...] = jnp.full(fxs.shape, fx_ref[0], I32)
    barrier = pltpu.get_barrier_semaphore()
    for d in range(1, nf):
        pl.semaphore_signal(barrier, inc=1, device_id=(partner(f, nf, d), c), device_id_type=MESH)
    for d in range(1, nc):
        pl.semaphore_signal(barrier, inc=1, device_id=(f, partner(c, nc, d)), device_id_type=MESH)

    start = c * width
    xs = lax.broadcasted_iota(I32, (ncol, width), 1) + start
    row = lax.broadcasted_iota(I32, (ncol, width), 0)
    uv = jnp.zeros((ncol, width), I32)
    for i in range(ncol):
        uv = jnp.where(row == i, u_ref[i], uv)
    pc, ps = turn((2 * uv + (SG - 1)) * xs, mod)
    premod[0] = pc
    premod[1] = ps
    h_ref[...] = jnp.zeros_like(h_ref)
    pl.semaphore_wait(barrier, nf + nc - 2)

    small = []
    sends = []
    for d in range(1, nf):
        copy = pltpu.make_async_remote_copy(
            src_ref=fxs, dst_ref=fxall.at[f],
            send_sem=s_fx.at[d], recv_sem=r_fx.at[d],
            device_id=(partner(f, nf, d), c), device_id_type=MESH,
        )
        copy.start()
        small.append(copy)
    copy = pltpu.make_async_copy(fxs, fxall.at[f], l_sem.at[len(cuts)])
    copy.start()
    small.append(copy)
    for n, (y0, ny) in enumerate(cuts):
        group = []
        for d in range(1, nf):
            peer = partner(f, nf, d)
            copy = pltpu.make_async_remote_copy(
                src_ref=facets_ref.at[pl.ds(peer * rpd + y0, ny)],
                dst_ref=cells.at[pl.ds(y0, ny), :, f],
                send_sem=s_a2a.at[n, d], recv_sem=r_a2a.at[n, d],
                device_id=(peer, c), device_id_type=MESH,
            )
            copy.start()
            group.append(copy)
        copy = pltpu.make_async_copy(
            facets_ref.at[pl.ds(f * rpd + y0, ny)], cells.at[pl.ds(y0, ny), :, f], l_sem.at[n]
        )
        copy.start()
        group.append(copy)
        sends.append(group)

    block = 64

    def table_step(i, carry):
        first = pl.multiple_of(i * block, block)
        x = lax.broadcasted_iota(I32, (block, HALF), 0) + (start + first)
        j = lax.broadcasted_iota(I32, (block, HALF), 1)
        cosine, sine = turn((2 * j + 1) * x, mod)
        ch, cl = split(cosine)
        sh, sl = split(sine)
        table[0, pl.ds(first, block), pl.ds(0, HALF)] = ch
        table[0, pl.ds(first, block), pl.ds(HALF, HALF)] = sh
        table[1, pl.ds(first, block), pl.ds(0, HALF)] = cl
        table[1, pl.ds(first, block), pl.ds(HALF, HALF)] = sl
        return carry

    lax.fori_loop(0, width // block, table_step, 0)

    for copy in small:
        copy.wait()
    fx = fxall[:, 0, :]
    fx = jnp.concatenate([fx] * (SG // fx.shape[-1]), axis=1)
    lane = lax.broadcasted_iota(I32, (nf, SG), 1)
    a = jnp.where(lane < HALF, HALF + lane, SG - 1 - lane)

    def phase_step(i, carry):
        wc, ws = turn(2 * (a + u_ref[i]) * fx, mod)
        phase[0, i] = wc
        phase[1, i] = ws
        return carry

    lax.fori_loop(0, ncol, phase_step, 0)

    def transform(n):
        y0, ny = cuts[n]
        size = ny * nf
        for d in list(range(nc - 1, 0, -1)) + [0]:
            owner = partner(c, nc, d)
            for s in range(COLS_DEV):
                col = owner * COLS_DEV + s
                cosine = premod[0, pl.ds(col, 1), :].reshape(1, 1, width)
                sine = premod[1, pl.ds(col, 1), :].reshape(1, 1, width)
                re = cells[pl.ds(y0, ny), 0]
                im = cells[pl.ds(y0, ny), 1]
                zr = (re * cosine + im * sine).reshape(size, width)
                zi = (im * cosine - re * sine).reshape(size, width)
                for m, z in enumerate((zr, zi)):
                    hi, lo = split(z)
                    at = (s * 2 + m) * size
                    zbuf[0, pl.ds(at, size), :] = hi
                    zbuf[1, pl.ds(at, size), :] = lo
            every = pl.ds(0, 2 * COLS_DEV * size)
            high = zbuf[0, every, :]
            prod = mm(high, table[0]) + mm(zbuf[1, every, :], table[0]) + mm(high, table[1])
            for s in range(COLS_DEV):
                col = owner * COLS_DEV + s
                at = s * 2 * size
                fr = prod[at:at + size]
                fi = prod[at + size:at + 2 * size]
                rc, rs = fr[:, :HALF], fr[:, HALF:]
                ic, is_ = fi[:, :HALF], fi[:, HALF:]
                hr = jnp.concatenate([rc + is_, rc - is_], axis=1).reshape(ny, nf, SG)
                hm = jnp.concatenate([ic - rs, ic + rs], axis=1).reshape(ny, nf, SG)
                wc = phase[0, col]
                ws = phase[1, col]
                part[n, d, pl.ds(s * ny, ny), pl.ds(0, SG)] = jnp.sum(hr * wc + hm * ws, axis=1)
                part[n, d, pl.ds(s * ny, ny), pl.ds(SG, SG)] = jnp.sum(hm * wc - hr * ws, axis=1)
            if d:
                copy = pltpu.make_async_remote_copy(
                    src_ref=part.at[n, d], dst_ref=zrecv.at[n, d],
                    send_sem=s_z.at[n, d], recv_sem=r_z.at[n, d],
                    device_id=(f, owner), device_id_type=MESH,
                )
                copy.start()
                zcopies[n].append((d, copy))

    scale = 1.0 / math.sqrt(1.0 * rows * width * nc * nf)

    def v_step(i, carry):
        first = pl.multiple_of(i * block, block)
        b = lax.broadcasted_iota(I32, (block, depth), 0) + first
        q = lax.broadcasted_iota(I32, (block, depth), 1)
        inner = lax.rem(q, hpad)
        peer = lax.rem(lax.div(q, hpad), nf)
        piece = lax.div(q, hpad * nf)
        g = peer * rpd + inner
        for n, (y0, ny) in enumerate(cuts):
            g = jnp.where(piece == n, g + y0, g)
        cell = jnp.where(g < band, fy_ref[0] + g, fy_ref[1] + g - band)
        cosine, sine = turn(2 * (sv_ref[f] + b) * cell, mod)
        wide = jnp.concatenate([cosine, sine], axis=1) * F32(scale)
        hi, lo = split(wide)
        e_ref[pl.ds(first, block), pl.ds(0, 2 * depth)] = hi
        e_ref[pl.ds(first, block), pl.ds(2 * depth, 2 * depth)] = lo
        e_ref[pl.ds(first, block), pl.ds(4 * depth, 2 * depth)] = hi
        return carry

    zcopies = [[] for _ in cuts]
    for n in range(len(cuts)):
        for copy in sends[n]:
            copy.wait()
        transform(n)
    lax.fori_loop(0, SG // block, v_step, 0)

    flip = lax.broadcasted_iota(I32, (HALF, HALF), 0) + lax.broadcasted_iota(I32, (HALF, HALF), 1)
    flip = jnp.where(flip == HALF - 1, F32(1.0), F32(0.0)).astype(BF16)
    gcopies = []
    for n, (y0, ny) in enumerate(cuts):
        acc = part[n, 0]
        for d, copy in zcopies[n]:
            copy.wait()
            acc = acc + zrecv[n, d]
        pieces = []
        for m in range(2):
            hi, lo = split(acc[:, m * SG + HALF:(m + 1) * SG])
            pieces += [mm(hi, flip) + mm(lo, flip), acc[:, m * SG:m * SG + HALF]]
        total = jnp.concatenate(pieces, axis=1)
        options = [total[s * ny:(s + 1) * ny] for s in range(COLS_DEV)]
        group = []
        for d in range(1, nf):
            peer = partner(f, nf, d)
            chosen = options[0]
            for s in range(1, COLS_DEV):
                chosen = jnp.where(sc_ref[peer] == s, options[s], chosen)
            gsend[n, d, pl.ds(0, ny), :] = chosen
            copy = pltpu.make_async_remote_copy(
                src_ref=gsend.at[n, d], dst_ref=gat.at[n, f],
                send_sem=s_g.at[n, d], recv_sem=r_g.at[n, d],
                device_id=(peer, c), device_id_type=MESH,
            )
            copy.start()
            gcopies.append(copy)
        chosen = options[0]
        for s in range(1, COLS_DEV):
            chosen = jnp.where(sc_ref[f] == s, options[s], chosen)
        gat[n, f, pl.ds(0, ny), :] = chosen
    for copy in gcopies:
        copy.wait()
    for n, (y0, ny) in enumerate(cuts):
        for j in range(nf):
            h_ref[pl.ds((n * nf + j) * hpad, ny), :] = gat[n, j, pl.ds(0, ny), :]


def v_kernel(h_ref, e_ref, out_ref, rhs):
    @pl.when(pl.program_id(0) == 0)
    def _():
        k = h_ref.shape[0]
        hi, lo = split(h_ref[...])
        for n, h in enumerate((hi, hi, lo)):
            rhs[pl.ds(2 * n * k, k), :] = h
            rhs[pl.ds((2 * n + 1) * k, k), pl.ds(0, SG)] = h[:, SG:]
            rhs[pl.ds((2 * n + 1) * k, k), pl.ds(SG, SG)] = -h[:, :SG]

    out_ref[...] = mm(e_ref[...], rhs[...])


def per_device(nf, nc, facets, facet_x, facet_y, col_u, slot_col, slot_v):
    width = facets.shape[-1]
    band = facets.shape[2]
    img = width * nc * nf
    rows = facets.shape[0] * band
    rpd = rows // nf
    ncol = COLS_DEV * nc
    cuts = ((0, rpd // 2), (rpd // 2, rpd - rpd // 2))
    most = rpd - rpd // 2
    hpad = 1 << (most - 1).bit_length()
    depth = len(cuts) * nf * hpad
    pieces = len(cuts)
    vm = pl.BlockSpec(memory_space=pltpu.VMEM)
    sm = pl.BlockSpec(memory_space=pltpu.SMEM)
    dma = pltpu.SemaphoreType.DMA
    h, e = pl.pallas_call(
        functools.partial(gather_kernel, nf, nc, img, band, cuts, hpad),
        out_shape=(
            jax.ShapeDtypeStruct((depth, 2 * SG), F32),
            jax.ShapeDtypeStruct((SG, 6 * depth), BF16),
        ),
        in_specs=[sm, sm, sm, sm, sm, pl.BlockSpec(memory_space=pltpu.HBM)],
        out_specs=(vm, vm),
        scratch_shapes=[
            pltpu.VMEM((rpd, 2, nf, width), F32),
            pltpu.VMEM((8, 128), I32),
            pltpu.VMEM((nf, 8, 128), I32),
            pltpu.VMEM((2, width, SG), BF16),
            pltpu.VMEM((2, ncol, width), F32),
            pltpu.VMEM((2, ncol, nf, SG), F32),
            pltpu.VMEM((2, 2 * COLS_DEV * most * nf, width), BF16),
            pltpu.VMEM((pieces, nc, COLS_DEV * most, 2 * SG), F32),
            pltpu.VMEM((pieces, nc, COLS_DEV * most, 2 * SG), F32),
            pltpu.VMEM((pieces, nf, most, 2 * SG), F32),
            pltpu.VMEM((pieces, nf, most, 2 * SG), F32),
            dma((pieces, nf)), dma((pieces, nf)), dma((nf,)), dma((nf,)),
            dma((pieces, nc)), dma((pieces, nc)), dma((pieces, nf)), dma((pieces, nf)),
            dma((pieces + 1,)),
        ],
        compiler_params=pltpu.CompilerParams(
            collective_id=0, has_side_effects=True, vmem_limit_bytes=24 << 20
        ),
        name="gather_columns",
    )(facet_x, facet_y, col_u, slot_col[0], slot_v[0], facets.reshape(rows, 2, width))
    tile = 128
    out = pl.pallas_call(
        v_kernel,
        grid=(SG // tile,),
        out_shape=jax.ShapeDtypeStruct((SG, 2 * SG), F32),
        in_specs=[
            pl.BlockSpec((depth, 2 * SG), lambda i: (0, 0)),
            pl.BlockSpec((tile, 6 * depth), lambda i: (i, 0)),
        ],
        out_specs=pl.BlockSpec((tile, 2 * SG), lambda i: (i, 0)),
        scratch_shapes=[pltpu.VMEM((6 * depth, 2 * SG), BF16)],
        compiler_params=pltpu.CompilerParams(vmem_limit_bytes=24 << 20),
        name="v_transform",
    )(h, e)
    return out[None, None]


def solution(mesh):
    placed = (
        P(None, "facet", None, None, "col"),
        P("facet"),
        P(),
        P(),
        P("col", None),
        P("col", None),
    )
    return jax.shard_map(
        functools.partial(per_device, mesh.shape["facet"], mesh.shape["col"]),
        mesh=mesh,
        in_specs=placed,
        out_specs=P("col", "facet", None, None),
        check_vma=False,
    )
```

```python
import functools
import math

import jax
import jax.numpy as jnp
from jax import lax
from jax.experimental import pallas as pl
from jax.experimental.pallas import tpu as pltpu
from jax.sharding import PartitionSpec as P

SG = 512
HALF = SG // 2
COLS_DEV = 2
F32 = jnp.float32
BF16 = jnp.bfloat16
I32 = jnp.int32
MESH = pl.DeviceIdType.MESH


def turn(m, mod):
    bits = mod.bit_length() - 1
    m = m & (mod - 1)
    quad = lax.shift_right_logical(m + (mod >> 3), jnp.int32(bits - 2))
    rest = m - lax.shift_left(quad, jnp.int32(bits - 2))
    t = rest.astype(F32) * F32(2.0 * math.pi / mod)
    t2 = t * t
    sine = t + t * t2 * (F32(-1 / 6) + t2 * (F32(1 / 120) + t2 * F32(-1 / 5040)))
    cosine = F32(1.0) + t2 * (
        F32(-0.5) + t2 * (F32(1 / 24) + t2 * (F32(-1 / 720) + t2 * F32(1 / 40320)))
    )
    odd = (quad & 1) == 1
    c = jnp.where(odd, sine, cosine)
    s = jnp.where(odd, cosine, sine)
    c = jnp.where(((quad + 1) & 2) == 2, -c, c)
    s = jnp.where((quad & 2) == 2, -s, s)
    return c, s


def split(value):
    high = value.astype(BF16)
    return high, (value - high.astype(F32)).astype(BF16)


def mm(a, b):
    return jnp.dot(a, b, preferred_element_type=F32)


def partner(index, count, step):
    if count & (count - 1):
        return lax.rem(index + step, count)
    bit = 1
    while bit < count:
        if step & bit:
            index = index + bit - 2 * bit * lax.rem(lax.div(index, bit), 2)
        bit *= 2
    return index


def gather_kernel(
    nf, nc, img, band, cuts, hpad,
    fx_ref, fy_hbm, u_hbm, sc_hbm, sv_hbm, facets_ref,
    h_ref, e_ref,
    cells, fxs, fxall, table, premod, phase, zbuf, part, zrecv, gsend, gat,
    fy_ref, u_ref, sc_ref, sv_ref,
    s_a2a, r_a2a, s_fx, r_fx, s_z, r_z, s_g, r_g, l_sem, i_sem,
):
    f = lax.axis_index("facet")
    c = lax.axis_index("col")
    rows = facets_ref.shape[0]
    rpd = rows // nf
    width = facets_ref.shape[-1]
    mod = 2 * img
    ncol = COLS_DEV * nc
    depth = len(cuts) * nf * hpad

    numbers = []
    for i, (src, dst) in enumerate((
        (fy_hbm, fy_ref), (u_hbm, u_ref), (sc_hbm, sc_ref), (sv_hbm, sv_ref)
    )):
        copy = pltpu.make_async_copy(src, dst, i_sem.at[i])
        copy.start()
        numbers.append(copy)
    barrier = pltpu.get_barrier_semaphore()
    for d in range(1, nf):
        pl.semaphore_signal(barrier, inc=1, device_id=(partner(f, nf, d), c), device_id_type=MESH)
    for d in range(1, nc):
        pl.semaphore_signal(barrier, inc=1, device_id=(f, partner(c, nc, d)), device_id_type=MESH)

    for copy in numbers:
        copy.wait()
    fxs[...] = jnp.full(fxs.shape, fx_ref[0], I32)
    start = c * width
    xs = lax.broadcasted_iota(I32, (ncol, width), 1) + start
    row = lax.broadcasted_iota(I32, (ncol, width), 0)
    uv = jnp.zeros((ncol, width), I32)
    for i in range(ncol):
        uv = jnp.where(row == i, u_ref[i], uv)
    pc, ps = turn((2 * uv + (SG - 1)) * xs, mod)
    premod[0] = pc
    premod[1] = ps
    h_ref[...] = jnp.zeros_like(h_ref)
    pl.semaphore_wait(barrier, nf + nc - 2)

    small = []
    sends = []
    for d in range(1, nf):
        copy = pltpu.make_async_remote_copy(
            src_ref=fxs, dst_ref=fxall.at[f],
            send_sem=s_fx.at[d], recv_sem=r_fx.at[d],
            device_id=(partner(f, nf, d), c), device_id_type=MESH,
        )
        copy.start()
        small.append(copy)
    copy = pltpu.make_async_copy(fxs, fxall.at[f], l_sem.at[len(cuts)])
    copy.start()
    small.append(copy)
    for n, (y0, ny) in enumerate(cuts):
        group = []
        for d in range(1, nf):
            peer = partner(f, nf, d)
            copy = pltpu.make_async_remote_copy(
                src_ref=facets_ref.at[pl.ds(peer * rpd + y0, ny)],
                dst_ref=cells.at[pl.ds(y0, ny), :, f],
                send_sem=s_a2a.at[n, d], recv_sem=r_a2a.at[n, d],
                device_id=(peer, c), device_id_type=MESH,
            )
            copy.start()
            group.append(copy)
        copy = pltpu.make_async_copy(
            facets_ref.at[pl.ds(f * rpd + y0, ny)], cells.at[pl.ds(y0, ny), :, f], l_sem.at[n]
        )
        copy.start()
        group.append(copy)
        sends.append(group)

    block = 64

    def table_step(i, carry):
        first = pl.multiple_of(i * block, block)
        x = lax.broadcasted_iota(I32, (block, HALF), 0) + (start + first)
        j = lax.broadcasted_iota(I32, (block, HALF), 1)
        cosine, sine = turn((2 * j + 1) * x, mod)
        ch, cl = split(cosine)
        sh, sl = split(sine)
        table[0, pl.ds(first, block), pl.ds(0, HALF)] = ch
        table[0, pl.ds(first, block), pl.ds(HALF, HALF)] = sh
        table[1, pl.ds(first, block), pl.ds(0, HALF)] = cl
        table[1, pl.ds(first, block), pl.ds(HALF, HALF)] = sl
        return carry

    lax.fori_loop(0, width // block, table_step, 0)

    for copy in small:
        copy.wait()
    fx = fxall[:, 0, :]
    fx = jnp.concatenate([fx] * (SG // fx.shape[-1]), axis=1)
    lane = lax.broadcasted_iota(I32, (nf, SG), 1)
    a = jnp.where(lane < HALF, HALF + lane, SG - 1 - lane)

    def phase_step(i, carry):
        wc, ws = turn(2 * (a + u_ref[i]) * fx, mod)
        phase[0, i] = wc
        phase[1, i] = ws
        return carry

    lax.fori_loop(0, ncol, phase_step, 0)

    def transform(n):
        y0, ny = cuts[n]
        size = ny * nf
        for d in list(range(nc - 1, 0, -1)) + [0]:
            owner = partner(c, nc, d)
            for s in range(COLS_DEV):
                col = owner * COLS_DEV + s
                cosine = premod[0, pl.ds(col, 1), :].reshape(1, 1, width)
                sine = premod[1, pl.ds(col, 1), :].reshape(1, 1, width)
                re = cells[pl.ds(y0, ny), 0]
                im = cells[pl.ds(y0, ny), 1]
                zr = (re * cosine + im * sine).reshape(size, width)
                zi = (im * cosine - re * sine).reshape(size, width)
                for m, z in enumerate((zr, zi)):
                    hi, lo = split(z)
                    at = (s * 2 + m) * size
                    zbuf[0, pl.ds(at, size), :] = hi
                    zbuf[1, pl.ds(at, size), :] = lo
            every = pl.ds(0, 2 * COLS_DEV * size)
            high = zbuf[0, every, :]
            prod = mm(high, table[0]) + mm(zbuf[1, every, :], table[0]) + mm(high, table[1])
            for s in range(COLS_DEV):
                col = owner * COLS_DEV + s
                at = s * 2 * size
                fr = prod[at:at + size]
                fi = prod[at + size:at + 2 * size]
                rc, rs = fr[:, :HALF], fr[:, HALF:]
                ic, is_ = fi[:, :HALF], fi[:, HALF:]
                hr = jnp.concatenate([rc + is_, rc - is_], axis=1).reshape(ny, nf, SG)
                hm = jnp.concatenate([ic - rs, ic + rs], axis=1).reshape(ny, nf, SG)
                wc = phase[0, col]
                ws = phase[1, col]
                part[n, d, pl.ds(s * ny, ny), pl.ds(0, SG)] = jnp.sum(hr * wc + hm * ws, axis=1)
                part[n, d, pl.ds(s * ny, ny), pl.ds(SG, SG)] = jnp.sum(hm * wc - hr * ws, axis=1)
            if d:
                copy = pltpu.make_async_remote_copy(
                    src_ref=part.at[n, d], dst_ref=zrecv.at[n, d],
                    send_sem=s_z.at[n, d], recv_sem=r_z.at[n, d],
                    device_id=(f, owner), device_id_type=MESH,
                )
                copy.start()
                zcopies[n].append((d, copy))

    scale = 1.0 / math.sqrt(1.0 * rows * width * nc * nf)

    def v_step(i, carry):
        first = pl.multiple_of(i * block, block)
        b = lax.broadcasted_iota(I32, (block, depth), 0) + first
        q = lax.broadcasted_iota(I32, (block, depth), 1)
        inner = lax.rem(q, hpad)
        peer = lax.rem(lax.div(q, hpad), nf)
        piece = lax.div(q, hpad * nf)
        g = peer * rpd + inner
        for n, (y0, ny) in enumerate(cuts):
            g = jnp.where(piece == n, g + y0, g)
        cell = jnp.where(g < band, fy_ref[0] + g, fy_ref[1] + g - band)
        cosine, sine = turn(2 * (sv_ref[f] + b) * cell, mod)
        wide = jnp.concatenate([cosine, sine], axis=1) * F32(scale)
        hi, lo = split(wide)
        e_ref[pl.ds(first, block), pl.ds(0, 2 * depth)] = hi
        e_ref[pl.ds(first, block), pl.ds(2 * depth, 2 * depth)] = lo
        e_ref[pl.ds(first, block), pl.ds(4 * depth, 2 * depth)] = hi
        return carry

    zcopies = [[] for _ in cuts]
    for n in range(len(cuts)):
        for copy in sends[n]:
            copy.wait()
        transform(n)
    lax.fori_loop(0, SG // block, v_step, 0)

    flip = lax.broadcasted_iota(I32, (HALF, HALF), 0) + lax.broadcasted_iota(I32, (HALF, HALF), 1)
    flip = jnp.where(flip == HALF - 1, F32(1.0), F32(0.0)).astype(BF16)
    gcopies = []
    for n, (y0, ny) in enumerate(cuts):
        acc = part[n, 0]
        for d, copy in zcopies[n]:
            copy.wait()
            acc = acc + zrecv[n, d]
        pieces = []
        for m in range(2):
            hi, lo = split(acc[:, m * SG + HALF:(m + 1) * SG])
            pieces += [mm(hi, flip) + mm(lo, flip), acc[:, m * SG:m * SG + HALF]]
        total = jnp.concatenate(pieces, axis=1)
        options = [total[s * ny:(s + 1) * ny] for s in range(COLS_DEV)]
        group = []
        for d in range(1, nf):
            peer = partner(f, nf, d)
            chosen = options[0]
            for s in range(1, COLS_DEV):
                chosen = jnp.where(sc_ref[peer] == s, options[s], chosen)
            gsend[n, d, pl.ds(0, ny), :] = chosen
            copy = pltpu.make_async_remote_copy(
                src_ref=gsend.at[n, d], dst_ref=gat.at[n, f],
                send_sem=s_g.at[n, d], recv_sem=r_g.at[n, d],
                device_id=(peer, c), device_id_type=MESH,
            )
            copy.start()
            gcopies.append(copy)
        chosen = options[0]
        for s in range(1, COLS_DEV):
            chosen = jnp.where(sc_ref[f] == s, options[s], chosen)
        gat[n, f, pl.ds(0, ny), :] = chosen
    for copy in gcopies:
        copy.wait()
    for n, (y0, ny) in enumerate(cuts):
        for j in range(nf):
            h_ref[pl.ds((n * nf + j) * hpad, ny), :] = gat[n, j, pl.ds(0, ny), :]


def v_kernel(h_ref, e_ref, out_ref, rhs):
    @pl.when(pl.program_id(0) == 0)
    def _():
        k = h_ref.shape[0]
        hi, lo = split(h_ref[...])
        for n, h in enumerate((hi, hi, lo)):
            rhs[pl.ds(2 * n * k, k), :] = h
            rhs[pl.ds((2 * n + 1) * k, k), pl.ds(0, SG)] = h[:, SG:]
            rhs[pl.ds((2 * n + 1) * k, k), pl.ds(SG, SG)] = -h[:, :SG]

    out_ref[...] = mm(e_ref[...], rhs[...])


def per_device(nf, nc, facets, facet_x, facet_y, col_u, slot_col, slot_v):
    width = facets.shape[-1]
    band = facets.shape[2]
    img = width * nc * nf
    rows = facets.shape[0] * band
    rpd = rows // nf
    ncol = COLS_DEV * nc
    cuts = ((0, rpd // 2), (rpd // 2, rpd - rpd // 2))
    most = rpd - rpd // 2
    hpad = 1 << (most - 1).bit_length()
    depth = len(cuts) * nf * hpad
    pieces = len(cuts)
    vm = pl.BlockSpec(memory_space=pltpu.VMEM)
    dma = pltpu.SemaphoreType.DMA
    h, e = pl.pallas_call(
        functools.partial(gather_kernel, nf, nc, img, band, cuts, hpad),
        out_shape=(
            jax.ShapeDtypeStruct((depth, 2 * SG), F32),
            jax.ShapeDtypeStruct((SG, 6 * depth), BF16),
        ),
        in_specs=[pl.BlockSpec(memory_space=pltpu.SMEM)] + [pl.BlockSpec(memory_space=pltpu.HBM)] * 5,
        out_specs=(vm, vm),
        scratch_shapes=[
            pltpu.VMEM((rpd, 2, nf, width), F32),
            pltpu.VMEM((8, 128), I32),
            pltpu.VMEM((nf, 8, 128), I32),
            pltpu.VMEM((2, width, SG), BF16),
            pltpu.VMEM((2, ncol, width), F32),
            pltpu.VMEM((2, ncol, nf, SG), F32),
            pltpu.VMEM((2, 2 * COLS_DEV * most * nf, width), BF16),
            pltpu.VMEM((pieces, nc, COLS_DEV * most, 2 * SG), F32),
            pltpu.VMEM((pieces, nc, COLS_DEV * most, 2 * SG), F32),
            pltpu.VMEM((pieces, nf, most, 2 * SG), F32),
            pltpu.VMEM((pieces, nf, most, 2 * SG), F32),
            pltpu.SMEM((2,), I32), pltpu.SMEM((ncol,), I32),
            pltpu.SMEM((nf,), I32), pltpu.SMEM((nf,), I32),
            dma((pieces, nf)), dma((pieces, nf)), dma((nf,)), dma((nf,)),
            dma((pieces, nc)), dma((pieces, nc)), dma((pieces, nf)), dma((pieces, nf)),
            dma((pieces + 1,)), dma((4,)),
        ],
        compiler_params=pltpu.CompilerParams(
            collective_id=0, has_side_effects=True, vmem_limit_bytes=24 << 20
        ),
        name="gather_columns",
    )(facet_x, *(
        pltpu.with_memory_space_constraint(z, pltpu.HBM)
        for z in (facet_y, col_u, slot_col[0], slot_v[0], facets.reshape(rows, 2, width))
    ))
    tile = 128
    out = pl.pallas_call(
        v_kernel,
        grid=(SG // tile,),
        out_shape=jax.ShapeDtypeStruct((SG, 2 * SG), F32),
        in_specs=[
            pl.BlockSpec((depth, 2 * SG), lambda i: (0, 0)),
            pl.BlockSpec((tile, 6 * depth), lambda i: (i, 0)),
        ],
        out_specs=pl.BlockSpec((tile, 2 * SG), lambda i: (i, 0)),
        scratch_shapes=[pltpu.VMEM((6 * depth, 2 * SG), BF16)],
        compiler_params=pltpu.CompilerParams(vmem_limit_bytes=24 << 20),
        name="v_transform",
    )(h, e)
    return out[None, None]


def solution(mesh):
    placed = (
        P(None, "facet", None, None, "col"),
        P("facet"),
        P(),
        P(),
        P("col", None),
        P("col", None),
    )
    return jax.shard_map(
        functools.partial(per_device, mesh.shape["facet"], mesh.shape["col"]),
        mesh=mesh,
        in_specs=placed,
        out_specs=P("col", "facet", None, None),
        check_vma=False,
    )
```

```python
import functools
import math

import jax
import jax.numpy as jnp
from jax import lax
from jax.experimental import pallas as pl
from jax.experimental.pallas import tpu as pltpu
from jax.sharding import PartitionSpec as P

SG = 512
HALF = SG // 2
COLS_DEV = 2
F32 = jnp.float32
BF16 = jnp.bfloat16
I32 = jnp.int32
MESH = pl.DeviceIdType.MESH


def turn(m, mod):
    bits = mod.bit_length() - 1
    m = m & (mod - 1)
    quad = lax.shift_right_logical(m + (mod >> 3), jnp.int32(bits - 2))
    rest = m - lax.shift_left(quad, jnp.int32(bits - 2))
    t = rest.astype(F32) * F32(2.0 * math.pi / mod)
    t2 = t * t
    sine = t + t * t2 * (F32(-1 / 6) + t2 * (F32(1 / 120) + t2 * F32(-1 / 5040)))
    cosine = F32(1.0) + t2 * (
        F32(-0.5) + t2 * (F32(1 / 24) + t2 * (F32(-1 / 720) + t2 * F32(1 / 40320)))
    )
    odd = (quad & 1) == 1
    c = jnp.where(odd, sine, cosine)
    s = jnp.where(odd, cosine, sine)
    c = jnp.where(((quad + 1) & 2) == 2, -c, c)
    s = jnp.where((quad & 2) == 2, -s, s)
    return c, s


def split(value):
    high = value.astype(BF16)
    return high, (value - high.astype(F32)).astype(BF16)


def mm(a, b):
    return jnp.dot(a, b, preferred_element_type=F32)


def partner(index, count, step):
    if count & (count - 1):
        return lax.rem(index + step, count)
    bit = 1
    while bit < count:
        if step & bit:
            index = index + bit - 2 * bit * lax.rem(lax.div(index, bit), 2)
        bit *= 2
    return index


def gather_kernel(
    nf, nc, img, band, cuts, hpad,
    fx_ref, fy_hbm, u_hbm, sc_hbm, sv_hbm, facets_ref,
    h_ref, e_ref,
    cells, fxs, fxall, table, premod, phase, zbuf, part, zrecv, gsend, gat,
    fy_ref, u_ref, sc_ref, sv_ref,
    s_a2a, r_a2a, s_fx, r_fx, s_z, r_z, s_g, r_g, l_sem, i_sem,
):
    f = lax.axis_index("facet")
    c = lax.axis_index("col")
    rows = facets_ref.shape[0]
    rpd = rows // nf
    width = facets_ref.shape[-1]
    mod = 2 * img
    ncol = COLS_DEV * nc
    depth = len(cuts) * nf * hpad

    fxs[...] = jnp.full(fxs.shape, fx_ref[0], I32)
    numbers = []
    for i, (src, dst) in enumerate((
        (fy_hbm, fy_ref), (u_hbm, u_ref), (sc_hbm, sc_ref), (sv_hbm, sv_ref)
    )):
        copy = pltpu.make_async_copy(src, dst, i_sem.at[i])
        copy.start()
        numbers.append(copy)
    barrier = pltpu.get_barrier_semaphore()
    for d in range(1, nf):
        pl.semaphore_signal(barrier, inc=1, device_id=(partner(f, nf, d), c), device_id_type=MESH)
    for d in range(1, nc):
        pl.semaphore_signal(barrier, inc=1, device_id=(f, partner(c, nc, d)), device_id_type=MESH)

    pl.semaphore_wait(barrier, nf + nc - 2)

    small = []
    sends = []
    for d in range(1, nf):
        copy = pltpu.make_async_remote_copy(
            src_ref=fxs, dst_ref=fxall.at[f],
            send_sem=s_fx.at[d], recv_sem=r_fx.at[d],
            device_id=(partner(f, nf, d), c), device_id_type=MESH,
        )
        copy.start()
        small.append(copy)
    copy = pltpu.make_async_copy(fxs, fxall.at[f], l_sem.at[len(cuts)])
    copy.start()
    small.append(copy)
    for n, (y0, ny) in enumerate(cuts):
        group = []
        for d in range(1, nf):
            peer = partner(f, nf, d)
            copy = pltpu.make_async_remote_copy(
                src_ref=facets_ref.at[pl.ds(peer * rpd + y0, ny)],
                dst_ref=cells.at[pl.ds(y0, ny), :, f],
                send_sem=s_a2a.at[n, d], recv_sem=r_a2a.at[n, d],
                device_id=(peer, c), device_id_type=MESH,
            )
            copy.start()
            group.append(copy)
        copy = pltpu.make_async_copy(
            facets_ref.at[pl.ds(f * rpd + y0, ny)], cells.at[pl.ds(y0, ny), :, f], l_sem.at[n]
        )
        copy.start()
        group.append(copy)
        sends.append(group)

    for copy in numbers:
        copy.wait()
    start = c * width
    xs = lax.broadcasted_iota(I32, (ncol, width), 1) + start
    row = lax.broadcasted_iota(I32, (ncol, width), 0)
    uv = jnp.zeros((ncol, width), I32)
    for i in range(ncol):
        uv = jnp.where(row == i, u_ref[i], uv)
    pc, ps = turn((2 * uv + (SG - 1)) * xs, mod)
    premod[0] = pc
    premod[1] = ps
    h_ref[...] = jnp.zeros_like(h_ref)
    block = 64

    def table_step(i, carry):
        first = pl.multiple_of(i * block, block)
        x = lax.broadcasted_iota(I32, (block, HALF), 0) + (start + first)
        j = lax.broadcasted_iota(I32, (block, HALF), 1)
        cosine, sine = turn((2 * j + 1) * x, mod)
        ch, cl = split(cosine)
        sh, sl = split(sine)
        table[0, pl.ds(first, block), pl.ds(0, HALF)] = ch
        table[0, pl.ds(first, block), pl.ds(HALF, HALF)] = sh
        table[1, pl.ds(first, block), pl.ds(0, HALF)] = cl
        table[1, pl.ds(first, block), pl.ds(HALF, HALF)] = sl
        return carry

    lax.fori_loop(0, width // block, table_step, 0)

    for copy in small:
        copy.wait()
    fx = fxall[:, 0, :]
    fx = jnp.concatenate([fx] * (SG // fx.shape[-1]), axis=1)
    lane = lax.broadcasted_iota(I32, (nf, SG), 1)
    a = jnp.where(lane < HALF, HALF + lane, SG - 1 - lane)

    def phase_step(i, carry):
        wc, ws = turn(2 * (a + u_ref[i]) * fx, mod)
        phase[0, i] = wc
        phase[1, i] = ws
        return carry

    lax.fori_loop(0, ncol, phase_step, 0)

    def transform(n):
        y0, ny = cuts[n]
        size = ny * nf
        for d in list(range(nc - 1, 0, -1)) + [0]:
            owner = partner(c, nc, d)
            for s in range(COLS_DEV):
                col = owner * COLS_DEV + s
                cosine = premod[0, pl.ds(col, 1), :].reshape(1, 1, width)
                sine = premod[1, pl.ds(col, 1), :].reshape(1, 1, width)
                re = cells[pl.ds(y0, ny), 0]
                im = cells[pl.ds(y0, ny), 1]
                zr = (re * cosine + im * sine).reshape(size, width)
                zi = (im * cosine - re * sine).reshape(size, width)
                for m, z in enumerate((zr, zi)):
                    hi, lo = split(z)
                    at = (s * 2 + m) * size
                    zbuf[0, pl.ds(at, size), :] = hi
                    zbuf[1, pl.ds(at, size), :] = lo
            every = pl.ds(0, 2 * COLS_DEV * size)
            high = zbuf[0, every, :]
            prod = mm(high, table[0]) + mm(zbuf[1, every, :], table[0]) + mm(high, table[1])
            for s in range(COLS_DEV):
                col = owner * COLS_DEV + s
                at = s * 2 * size
                fr = prod[at:at + size]
                fi = prod[at + size:at + 2 * size]
                rc, rs = fr[:, :HALF], fr[:, HALF:]
                ic, is_ = fi[:, :HALF], fi[:, HALF:]
                hr = jnp.concatenate([rc + is_, rc - is_], axis=1).reshape(ny, nf, SG)
                hm = jnp.concatenate([ic - rs, ic + rs], axis=1).reshape(ny, nf, SG)
                wc = phase[0, col]
                ws = phase[1, col]
                part[n, d, pl.ds(s * ny, ny), pl.ds(0, SG)] = jnp.sum(hr * wc + hm * ws, axis=1)
                part[n, d, pl.ds(s * ny, ny), pl.ds(SG, SG)] = jnp.sum(hm * wc - hr * ws, axis=1)
            if d:
                copy = pltpu.make_async_remote_copy(
                    src_ref=part.at[n, d], dst_ref=zrecv.at[n, d],
                    send_sem=s_z.at[n, d], recv_sem=r_z.at[n, d],
                    device_id=(f, owner), device_id_type=MESH,
                )
                copy.start()
                zcopies[n].append((d, copy))

    scale = 1.0 / math.sqrt(1.0 * rows * width * nc * nf)

    def v_step(i, carry):
        first = pl.multiple_of(i * block, block)
        b = lax.broadcasted_iota(I32, (block, depth), 0) + first
        q = lax.broadcasted_iota(I32, (block, depth), 1)
        inner = lax.rem(q, hpad)
        peer = lax.rem(lax.div(q, hpad), nf)
        piece = lax.div(q, hpad * nf)
        g = peer * rpd + inner
        for n, (y0, ny) in enumerate(cuts):
            g = jnp.where(piece == n, g + y0, g)
        cell = jnp.where(g < band, fy_ref[0] + g, fy_ref[1] + g - band)
        cosine, sine = turn(2 * (sv_ref[f] + b) * cell, mod)
        wide = jnp.concatenate([cosine, sine], axis=1) * F32(scale)
        hi, lo = split(wide)
        e_ref[pl.ds(first, block), pl.ds(0, 2 * depth)] = hi
        e_ref[pl.ds(first, block), pl.ds(2 * depth, 2 * depth)] = lo
        e_ref[pl.ds(first, block), pl.ds(4 * depth, 2 * depth)] = hi
        return carry

    zcopies = [[] for _ in cuts]
    for n in range(len(cuts)):
        for copy in sends[n]:
            copy.wait()
        transform(n)
    lax.fori_loop(0, SG // block, v_step, 0)

    flip = lax.broadcasted_iota(I32, (HALF, HALF), 0) + lax.broadcasted_iota(I32, (HALF, HALF), 1)
    flip = jnp.where(flip == HALF - 1, F32(1.0), F32(0.0)).astype(BF16)
    gcopies = []
    for n, (y0, ny) in enumerate(cuts):
        acc = part[n, 0]
        for d, copy in zcopies[n]:
            copy.wait()
            acc = acc + zrecv[n, d]
        pieces = []
        for m in range(2):
            hi, lo = split(acc[:, m * SG + HALF:(m + 1) * SG])
            pieces += [mm(hi, flip) + mm(lo, flip), acc[:, m * SG:m * SG + HALF]]
        total = jnp.concatenate(pieces, axis=1)
        options = [total[s * ny:(s + 1) * ny] for s in range(COLS_DEV)]
        group = []
        for d in range(1, nf):
            peer = partner(f, nf, d)
            chosen = options[0]
            for s in range(1, COLS_DEV):
                chosen = jnp.where(sc_ref[peer] == s, options[s], chosen)
            gsend[n, d, pl.ds(0, ny), :] = chosen
            copy = pltpu.make_async_remote_copy(
                src_ref=gsend.at[n, d], dst_ref=gat.at[n, f],
                send_sem=s_g.at[n, d], recv_sem=r_g.at[n, d],
                device_id=(peer, c), device_id_type=MESH,
            )
            copy.start()
            gcopies.append(copy)
        chosen = options[0]
        for s in range(1, COLS_DEV):
            chosen = jnp.where(sc_ref[f] == s, options[s], chosen)
        gat[n, f, pl.ds(0, ny), :] = chosen
    for copy in gcopies:
        copy.wait()
    for n, (y0, ny) in enumerate(cuts):
        for j in range(nf):
            h_ref[pl.ds((n * nf + j) * hpad, ny), :] = gat[n, j, pl.ds(0, ny), :]


def v_kernel(h_ref, e_ref, out_ref, rhs):
    @pl.when(pl.program_id(0) == 0)
    def _():
        k = h_ref.shape[0]
        hi, lo = split(h_ref[...])
        for n, h in enumerate((hi, hi, lo)):
            rhs[pl.ds(2 * n * k, k), :] = h
            rhs[pl.ds((2 * n + 1) * k, k), pl.ds(0, SG)] = h[:, SG:]
            rhs[pl.ds((2 * n + 1) * k, k), pl.ds(SG, SG)] = -h[:, :SG]

    out_ref[...] = mm(e_ref[...], rhs[...])


def per_device(nf, nc, facets, facet_x, facet_y, col_u, slot_col, slot_v):
    width = facets.shape[-1]
    band = facets.shape[2]
    img = width * nc * nf
    rows = facets.shape[0] * band
    rpd = rows // nf
    ncol = COLS_DEV * nc
    cuts = ((0, rpd // 2), (rpd // 2, rpd - rpd // 2))
    most = rpd - rpd // 2
    hpad = 1 << (most - 1).bit_length()
    depth = len(cuts) * nf * hpad
    pieces = len(cuts)
    vm = pl.BlockSpec(memory_space=pltpu.VMEM)
    dma = pltpu.SemaphoreType.DMA
    h, e = pl.pallas_call(
        functools.partial(gather_kernel, nf, nc, img, band, cuts, hpad),
        out_shape=(
            jax.ShapeDtypeStruct((depth, 2 * SG), F32),
            jax.ShapeDtypeStruct((SG, 6 * depth), BF16),
        ),
        in_specs=[pl.BlockSpec(memory_space=pltpu.SMEM)] + [pl.BlockSpec(memory_space=pltpu.HBM)] * 5,
        out_specs=(vm, vm),
        scratch_shapes=[
            pltpu.VMEM((rpd, 2, nf, width), F32),
            pltpu.VMEM((8, 128), I32),
            pltpu.VMEM((nf, 8, 128), I32),
            pltpu.VMEM((2, width, SG), BF16),
            pltpu.VMEM((2, ncol, width), F32),
            pltpu.VMEM((2, ncol, nf, SG), F32),
            pltpu.VMEM((2, 2 * COLS_DEV * most * nf, width), BF16),
            pltpu.VMEM((pieces, nc, COLS_DEV * most, 2 * SG), F32),
            pltpu.VMEM((pieces, nc, COLS_DEV * most, 2 * SG), F32),
            pltpu.VMEM((pieces, nf, most, 2 * SG), F32),
            pltpu.VMEM((pieces, nf, most, 2 * SG), F32),
            pltpu.SMEM((2,), I32), pltpu.SMEM((ncol,), I32),
            pltpu.SMEM((nf,), I32), pltpu.SMEM((nf,), I32),
            dma((pieces, nf)), dma((pieces, nf)), dma((nf,)), dma((nf,)),
            dma((pieces, nc)), dma((pieces, nc)), dma((pieces, nf)), dma((pieces, nf)),
            dma((pieces + 1,)), dma((4,)),
        ],
        compiler_params=pltpu.CompilerParams(
            collective_id=0, has_side_effects=True, vmem_limit_bytes=24 << 20
        ),
        name="gather_columns",
    )(facet_x, *(
        pltpu.with_memory_space_constraint(z, pltpu.HBM)
        for z in (facet_y, col_u, slot_col[0], slot_v[0], facets.reshape(rows, 2, width))
    ))
    tile = 128
    out = pl.pallas_call(
        v_kernel,
        grid=(SG // tile,),
        out_shape=jax.ShapeDtypeStruct((SG, 2 * SG), F32),
        in_specs=[
            pl.BlockSpec((depth, 2 * SG), lambda i: (0, 0)),
            pl.BlockSpec((tile, 6 * depth), lambda i: (i, 0)),
        ],
        out_specs=pl.BlockSpec((tile, 2 * SG), lambda i: (i, 0)),
        scratch_shapes=[pltpu.VMEM((6 * depth, 2 * SG), BF16)],
        compiler_params=pltpu.CompilerParams(vmem_limit_bytes=24 << 20),
        name="v_transform",
    )(h, e)
    return out[None, None]


def solution(mesh):
    placed = (
        P(None, "facet", None, None, "col"),
        P("facet"),
        P(),
        P(),
        P("col", None),
        P("col", None),
    )
    return jax.shard_map(
        functools.partial(per_device, mesh.shape["facet"], mesh.shape["col"]),
        mesh=mesh,
        in_specs=placed,
        out_specs=P("col", "facet", None, None),
        check_vma=False,
    )
```
